32 devices in a mesh: rel: 4 (over z), node: 8 (over y, x, core).
Axes of the slice: x: 2, y: 2, z: 4, core: 2. Of those that a mesh axis runs over, the one named last changes fastest.
Arguments:
- src_feat: bfloat16 [4, 8192, 768], P('rel', 'node'), may hold values from -6 to 6
- adj_tiles: bfloat16 [4, 128, 128, 128], P('rel', 'node'), may hold values from -0.0625 to 0.0625
- block_index: int32 [4, 8, 16], P('rel', 'node'), may hold values from 0 to 15, each once within a row
- block_live: int32 [4, 8, 16], P('rel', 'node'), may hold values from 0 to 1, as said below
- section_rel: int32 [4], replicated, may hold values from 0 to 2, as said below
- rel_weight: bfloat16 [3, 768, 1024], P(None, 'node'), may hold values from -0.109375 to 0.109375
- cotangent: bfloat16 [256, 1024], P('node', 'rel'), may hold values from -6 to 6
Outputs:
- joined: bfloat16 [256, 1024], P('node', 'rel')
- src_grad: bfloat16 [4, 8192, 768], P('rel', 'node')
- weight_grad: float32 [3, 768, 1024], P(None, 'node')
The draws below stay inside these ranges and needn't reach their ends.
Inputs may be any that keep to these rules, and one draw needn't show every extreme that they name: `block_index`: each device's list names every pair of a target block and a local source block once. `block_live`: sections differ in their share of live slots; in every draw some device has all 16 slots live. `section_rel`: every relation owns at least one section.
All inputs are finite; a program needn't handle non-finite values.
Results may differ from the reference program's by a relative error of at most 0.039.
Values may be sent and summed in bfloat16 or wider, within the bound.
No kernel may reach another device: no remote copies, remote signals or barrier semaphores. Data moves between devices by JAX's collectives and lax.ppermute only.
A program may use at most 64 MiB of HBM per device.

```python
import jax
import jax.numpy as jnp
from jax import lax

D_IN = 768
D_OUT = 1024
RELS = 3
BLOCK = 128
BATCHES = 2
TGT = 128
SRC_DEV = 1024
SECTIONS = 4
SRC = 8192
TT = 256
SB = 8
KB = 16
N_REL = 4
N_NODE = 8


def draw_block_live(key, part):
    keys = jax.random.split(jax.random.fold_in(key, 71), 4)
    live_level = jax.random.randint(keys[0], (SECTIONS, 1, 1), 2, KB + 1)
    draw_roll = jax.random.randint(keys[1], (SECTIONS, N_NODE, KB), 0, KB)
    alive_slots = draw_roll < live_level
    section_full = jax.random.randint(keys[2], (), 0, SECTIONS)
    node_full = jax.random.randint(keys[3], (), 0, N_NODE)
    forced = (jnp.arange(SECTIONS)[:, None, None] == section_full) & (jnp.arange(N_NODE)[None, :, None] == node_full)
    return jnp.where(forced | alive_slots, 1, 0).astype(jnp.int32)


def draw_section_rel(key, part):
    keys = jax.random.split(jax.random.fold_in(key, 53), 2)
    position = jnp.arange(SECTIONS)
    extra_draw = jax.random.randint(keys[0], (SECTIONS,), 0, 4)
    extra_rel = jnp.where(extra_draw == 3, 0, extra_draw)
    rel_of_pos = jnp.where(position < 3, position, extra_rel)
    shuffle = jax.random.permutation(keys[1], SECTIONS)
    return rel_of_pos[shuffle].astype(jnp.int32)


def levels(stream_key, dims, cuts, smallest, high):
    def one(dim, blocks):
        draws = jax.random.uniform(jax.random.fold_in(jax.random.fold_in(stream_key, 6), dim), (blocks,), jnp.float32, smallest / len(cuts), high / len(cuts))
        return jnp.repeat(jnp.exp(draws), dims[dim] // blocks).reshape((-1,) + (1,) * (len(dims) - dim - 1))

    loudness = one(*cuts[0])
    for cut in cuts[1:]:
        loudness = loudness * one(*cut)
    return loudness


def gaussian(rng, dims, width, most, cuts=(), kind=jnp.bfloat16):
    result = width * jax.random.normal(rng, dims, jnp.float32)
    if cuts:
        result = result * levels(rng, dims, cuts, -0.22, 0.18)
    return jnp.clip(result, -most, most).astype(kind)


def setup_inputs(seed: int = 0) -> dict:
    arg_keys = jax.random.split(jax.random.key(seed), 8)
    src_feat = gaussian(arg_keys[0], (SECTIONS, SRC, D_IN), 1.0, 6.0, ((0, 4), (1, 8)))
    adj_tiles = gaussian(arg_keys[1], (SECTIONS, N_NODE * KB, BLOCK, BLOCK), (BLOCK * SB * N_NODE) ** -0.5, 0.0625, ((0, 4), (1, 8)))
    block_index = jax.vmap(lambda own: jax.random.permutation(own, KB))(jax.random.split(arg_keys[2], SECTIONS * N_NODE)).reshape((SECTIONS, N_NODE, KB)).astype(jnp.int32)
    block_live = draw_block_live(jax.random.fold_in(arg_keys[7], 71), 0)
    section_rel = draw_section_rel(jax.random.fold_in(arg_keys[7], 71), 0)
    rel_weight = gaussian(arg_keys[5], (RELS, D_IN, D_OUT), (D_IN * N_REL) ** -0.5, 0.109375, ((1, 8),))
    cotangent = gaussian(arg_keys[6], (TT, D_OUT), 1.0, 6.0, ((0, 8), (1, 4)))
    return dict(src_feat=src_feat, adj_tiles=adj_tiles, block_index=block_index, block_live=block_live, section_rel=section_rel, rel_weight=rel_weight, cotangent=cotangent)


def gelu_tanh(value):
    return jax.nn.gelu(value, approximate=True)

def reference(src_feat, adj_tiles, block_index, block_live, section_rel, rel_weight, cotangent):
    highest = lax.Precision.HIGHEST
    src_count = SRC_DEV // BLOCK
    tgt_count = BATCHES * TGT // BLOCK
    all_targets = BATCHES * TGT
    features = src_feat.reshape(SECTIONS, N_NODE, src_count, BLOCK, D_IN)
    adj_blocks = adj_tiles.reshape(SECTIONS, N_NODE, KB, BLOCK, BLOCK)
    tgt_of = (block_index // src_count).astype(jnp.int32)
    src_of = (block_index % src_count).astype(jnp.int32)

    def forward_section(inputs):
        sec_feat, sec_adj, sec_tgt, sec_src, sec_live = inputs

        def node_step(total, shard):
            shard_feat, shard_adj, shard_tgt, shard_src, shard_live = shard
            gathered = shard_feat[shard_src].astype(jnp.float32)
            product = jnp.einsum('kij,kjd->kid', shard_adj.astype(jnp.float32), gathered, precision=highest)
            placing = ((shard_tgt[None, :] == jnp.arange(tgt_count, dtype=jnp.int32)[:, None]) & (shard_live[None, :] == 1)).astype(jnp.float32)
            return (total + jnp.einsum('tk,kid->tid', placing, product, precision=highest), None)
        total, _ = lax.scan(node_step, jnp.zeros((tgt_count, BLOCK, D_IN), jnp.float32), (sec_feat, sec_adj, sec_tgt, sec_src, sec_live))
        return total.reshape(all_targets, D_IN).astype(jnp.bfloat16)
    aggregate = lax.map(forward_section, (features, adj_blocks, tgt_of, src_of, block_live))
    chosen = rel_weight[section_rel]
    pre_act = jnp.einsum('std,sde->te', aggregate.astype(jnp.float32), chosen.astype(jnp.float32), precision=highest)
    joined = gelu_tanh(pre_act).astype(jnp.bfloat16)
    _, pullback = jax.vjp(gelu_tanh, pre_act)
    grad_pre = pullback(cotangent.astype(jnp.float32))[0].astype(jnp.bfloat16)
    agg_grad = jnp.einsum('te,sde->std', grad_pre.astype(jnp.float32), chosen.astype(jnp.float32), precision=highest).astype(jnp.bfloat16)
    grad_blocks = agg_grad.reshape(SECTIONS, tgt_count, BLOCK, D_IN)

    def backward_section(inputs):
        sec_grad, sec_adj, sec_tgt, sec_src, sec_live = inputs

        def node_back(carry, shard):
            shard_adj, shard_tgt, shard_src, shard_live = shard
            selected = sec_grad[shard_tgt].astype(jnp.float32)
            product = jnp.einsum('kij,kid->kjd', shard_adj.astype(jnp.float32), selected, precision=highest)
            placing = ((shard_src[None, :] == jnp.arange(src_count, dtype=jnp.int32)[:, None]) & (shard_live[None, :] == 1)).astype(jnp.float32)
            return (carry, jnp.einsum('sk,kjd->sjd', placing, product, precision=highest))
        _, grads = lax.scan(node_back, jnp.zeros((), jnp.float32), (sec_adj, sec_tgt, sec_src, sec_live))
        return grads.reshape(SRC_DEV * N_NODE, D_IN).astype(jnp.bfloat16)
    src_grad = lax.map(backward_section, (grad_blocks, adj_blocks, tgt_of, src_of, block_live))
    per_section = jnp.einsum('std,te->sde', aggregate.astype(jnp.float32), grad_pre.astype(jnp.float32), precision=highest)
    relation_onehot = (section_rel[:, None] == jnp.arange(RELS, dtype=jnp.int32)[None, :]).astype(jnp.float32)
    weight_grad = jnp.einsum('sr,sde->rde', relation_onehot, per_section, precision=highest)
    return (joined, src_grad, weight_grad)
```

```python
import functools

import jax
import jax.numpy as jnp
from jax import lax
from jax.experimental import pallas as pl
from jax.experimental.pallas import tpu as pltpu
from jax.sharding import PartitionSpec as P


F32 = jnp.float32
BF16 = jnp.bfloat16
VMEM = pl.BlockSpec(memory_space=pltpu.VMEM)
SMEM = pl.BlockSpec(memory_space=pltpu.SMEM)


def swap(value, axis, distance):
    size = lax.axis_size(axis)
    return lax.ppermute(value, axis, [(i, i ^ distance) for i in range(size)])


def tree_sum(values):
    while len(values) > 1:
        values = [values[i] + values[i + 1] for i in range(0, len(values), 2)]
    return values[0]


def call(body, out_shape, specs, *args, flops=0, nbytes=0, scratch=()):
    return pl.pallas_call(
        body,
        out_shape=out_shape,
        in_specs=specs,
        out_specs=jax.tree.map(lambda _: VMEM, out_shape),
        scratch_shapes=scratch,
        cost_estimate=pl.CostEstimate(flops=flops, bytes_accessed=nbytes, transcendentals=0),
    )(*args)


def pick_kernel(rel_ref, w_ref, out_ref, sem):
    mine = rel_ref[lax.axis_index("rel")]
    copy = pltpu.make_async_copy(w_ref.at[mine], out_ref, sem)
    copy.start()
    copy.wait()


def aggregate_kernel(index_ref, live_ref, tiles_ref, src_ref, keep_ref, send_ref, adj_ref):
    node = lax.axis_index("node")
    slots, block = tiles_ref.shape[1], tiles_ref.shape[2]
    chips, rows = keep_ref.shape[0], keep_ref.shape[1]
    per_tile = block // rows
    width = adj_ref.shape[2]
    src_count = width // block
    for slot in range(slots):
        where = index_ref[0, 0, slot]
        tgt = lax.div(where, src_count)
        column = pl.multiple_of(lax.rem(where, src_count) * block, block)
        live = live_ref[0, 0, slot] == 1
        tile = tiles_ref[0, slot]
        tile = jnp.where(live, tile, jnp.zeros_like(tile))
        for part in range(per_tile):
            apart = (tgt * per_tile + part) ^ node
            place = (apart & 1) * chips + (apart >> 1)
            adj_ref[place, :, pl.ds(column, block)] = tile[part * rows : (part + 1) * rows]
    src = src_ref[0]
    for ref, first in ((send_ref, chips), (keep_ref, 0)):
        lhs = adj_ref[first : first + chips].reshape(chips * rows, width)
        out = jnp.dot(lhs, src, preferred_element_type=F32)
        ref[...] = out.reshape(ref.shape).astype(ref.dtype)


def pair_kernel(keep_ref, got_ref, *outs):
    for j, out in enumerate(outs):
        out[...] = (keep_ref[j] + got_ref[j].astype(F32)).astype(out.dtype)


def place_weights(parts, w_ref):
    node = lax.axis_index("node")
    for m, part in enumerate(parts):
        w_ref[node ^ m] = part[...]
    return w_ref[...].reshape(w_ref.shape[0] * w_ref.shape[1], w_ref.shape[2])


def forward_kernel(chips, nodes, *refs):
    own, got, parts = refs[0], refs[1:chips], refs[chips : chips + nodes]
    y_ref, keep_ref, send_ref, w_ref, cols_ref = refs[chips + nodes :]
    node = lax.axis_index("node")
    total = own[...]
    for ref in got:
        total = total + ref[...].astype(F32)
    agg = total.astype(BF16)
    w = place_weights(parts, w_ref)
    y_ref[...] = jnp.dot(agg, w, preferred_element_type=F32).astype(BF16)
    width = keep_ref.shape[2]
    for i in range(nodes):
        cols_ref[i] = agg[:, i * width : (i + 1) * width]
    for j in range(chips):
        keep_ref[j] = cols_ref[node ^ (2 * j)]
        send_ref[j] = cols_ref[node ^ (2 * j + 1)]


def join_kernel(keep_ref, got_ref, *outs):
    for j, out in enumerate(outs):
        out[0] = keep_ref[j]
        out[1] = got_ref[j]


def gelu_tanh(value):
    return jax.nn.gelu(value, approximate=True)


def gelu_kernel(rels, *refs):
    ys, cots = refs[:rels], refs[rels : 2 * rels]
    joined_ref, grad_ref, cot_ref, out_ref = refs[2 * rels :]
    rel = lax.axis_index("rel")
    width = joined_ref.shape[1]
    pre = tree_sum([ref[...].astype(F32) for ref in ys])
    for d, ref in enumerate(cots):
        cot_ref[rel ^ d] = ref[...].astype(F32)
    cot = jnp.concatenate([cot_ref[i] for i in range(rels)], axis=1)
    scale = 0.7978845608028654
    square = pre * pre
    t = jnp.tanh(scale * (pre + 0.044715 * (square * pre)))
    half = 0.5 * (1.0 + t)
    joined = pre * half
    slope = half + 0.5 * pre * (1.0 - t * t) * (scale * (1.0 + 3 * 0.044715 * square))
    grad_ref[...] = (cot * slope).astype(BF16)
    for i in range(rels):
        out_ref[i] = joined[:, i * width : (i + 1) * width]
    joined_ref[...] = out_ref[rel].astype(BF16)


def backward_kernel(chips, nodes, rels, *refs):
    rel_ref, adj_ref = refs[:2]
    grads = refs[2 : 2 + nodes]
    parts = refs[2 + nodes : 2 + 2 * nodes]
    aggs = refs[2 + 2 * nodes : 2 + 2 * nodes + chips * rels]
    src_grad_ref, weight_grad_ref, w_ref, agg_ref = refs[2 + 2 * nodes + chips * rels :]
    rel = lax.axis_index("rel")
    order = [(q, j) for q in range(2) for j in range(chips)]
    grad = jnp.concatenate([grads[2 * j + q][...] for q, j in order], axis=0)
    w = place_weights(parts, w_ref)
    agg_grad = lax.dot_general(
        grad, w, (((1,), (1,)), ((), ())), preferred_element_type=F32
    ).astype(BF16)
    adj = adj_ref[...].reshape(adj_ref.shape[0] * adj_ref.shape[1], adj_ref.shape[2])
    src_grad_ref[0] = lax.dot_general(
        adj, agg_grad, (((0,), (0,)), ((), ())), preferred_element_type=F32
    ).astype(BF16)
    for d in range(rels):
        for i, (q, j) in enumerate(order):
            agg_ref[rel ^ d, i] = aggs[d * chips + j][q]
    weight_grad_ref[...] = jnp.zeros_like(weight_grad_ref)
    for section in range(rels):
        agg = agg_ref[section].reshape(grad.shape[0], agg_ref.shape[3])
        which = rel_ref[section]
        weight_grad_ref[which] += lax.dot_general(
            agg, grad, (((0,), (0,)), ((), ())), preferred_element_type=F32
        )


def local(src_feat, adj_tiles, block_index, block_live, section_rel, rel_weight, cotangent):
    nodes = lax.axis_size("node")
    rels = lax.axis_size("rel")
    chips = nodes // 2
    sources, in_width = src_feat.shape[1], src_feat.shape[2]
    relations, w_rows, out_width = rel_weight.shape
    rows, cot_width = cotangent.shape
    shape = jax.ShapeDtypeStruct
    any_spec = pl.BlockSpec(memory_space=pl.ANY)

    w_mine = call(
        pick_kernel,
        shape((w_rows, out_width), BF16),
        [SMEM, any_spec],
        section_rel,
        rel_weight,
        nbytes=4 * w_rows * out_width,
        scratch=[pltpu.SemaphoreType.DMA],
    )
    w_even = [w_mine] + [swap(w_mine, "node", 2 * j) for j in range(1, chips)]
    w_odd = [swap(part, "node", 1) for part in w_even]
    w_parts = [part for pair in zip(w_even, w_odd) for part in pair]

    keep, send, adj = call(
        aggregate_kernel,
        (
            shape((chips, rows, in_width), F32),
            shape((chips, rows, in_width), BF16),
            shape((nodes, rows, sources), BF16),
        ),
        [SMEM, SMEM, VMEM, VMEM],
        block_index,
        block_live,
        adj_tiles,
        src_feat,
        flops=2 * nodes * rows * sources * in_width,
        nbytes=4 * sources * in_width,
    )
    got = swap(send, "node", 1)
    halves = call(
        pair_kernel,
        tuple(shape((rows, in_width), F32 if j == 0 else BF16) for j in range(chips)),
        [VMEM, VMEM],
        keep,
        got,
        nbytes=8 * chips * rows * in_width,
    )
    arrived = [swap(halves[j], "node", 2 * j) for j in range(1, chips)]
    y, cols_keep, cols_send = call(
        functools.partial(forward_kernel, chips, nodes),
        (
            shape((rows, out_width), BF16),
            shape((chips, rows, w_rows), BF16),
            shape((chips, rows, w_rows), BF16),
        ),
        [VMEM] * (chips + nodes),
        halves[0],
        *arrived,
        *w_parts,
        flops=2 * rows * in_width * out_width,
        nbytes=4 * in_width * out_width,
        scratch=[
            pltpu.VMEM((nodes, w_rows, out_width), BF16),
            pltpu.VMEM((nodes, rows, w_rows), BF16),
        ],
    )
    ys = [y] + [swap(y, "rel", d) for d in range(1, rels)]
    cots = [cotangent] + [swap(cotangent, "rel", d) for d in range(1, rels)]

    cols_got = swap(cols_send, "node", 1)
    messages = call(
        join_kernel,
        tuple(shape((2, rows, w_rows), BF16) for _ in range(chips)),
        [VMEM, VMEM],
        cols_keep,
        cols_got,
        nbytes=8 * chips * rows * w_rows,
    )
    cols = [messages[0]] + [swap(messages[j], "node", 2 * j) for j in range(1, chips)]

    joined, grad = call(
        functools.partial(gelu_kernel, rels),
        (shape((rows, cot_width), BF16), shape((rows, out_width), BF16)),
        [VMEM] * (2 * rels),
        *ys,
        *cots,
        nbytes=4 * rels * rows * out_width,
        scratch=[
            pltpu.VMEM((rels, rows, cot_width), F32),
            pltpu.VMEM((rels, rows, cot_width), F32),
        ],
    )
    grads_even = [grad] + [swap(grad, "node", 2 * j) for j in range(1, chips)]
    grads_odd = [swap(part, "node", 1) for part in grads_even]
    grads = [part for pair in zip(grads_even, grads_odd) for part in pair]
    every = list(cols)
    for d in range(1, rels):
        every += [swap(part, "rel", d) for part in cols]

    src_grad, weight_grad = call(
        functools.partial(backward_kernel, chips, nodes, rels),
        (
            shape((1, sources, in_width), BF16),
            shape((relations, w_rows, out_width), F32),
        ),
        [SMEM, VMEM] + [VMEM] * (2 * nodes + chips * rels),
        section_rel,
        adj,
        *grads,
        *w_parts,
        *every,
        flops=4 * nodes * rows * sources * in_width,
        nbytes=8 * sources * in_width,
        scratch=[
            pltpu.VMEM((nodes, w_rows, out_width), BF16),
            pltpu.VMEM((rels, nodes, rows, w_rows), BF16),
        ],
    )
    return (joined, src_grad, weight_grad)


def solution(mesh):
    placed = (
        P("rel", "node", None),
        P("rel", "node", None, None),
        P("rel", "node", None),
        P("rel", "node", None),
        P(),
        P(None, "node", None),
        P("node", "rel"),
    )
    return jax.shard_map(
        local,
        mesh=mesh,
        in_specs=placed,
        out_specs=(P("node", "rel"), P("rel", "node", None), P(None, "node", None)),
        check_vma=False,
    )
```
